32 devices in a mesh: row: 8 (over z, core), col: 4 (over y, x).
Axes of the slice: x: 2, y: 2, z: 4, core: 2. Of those that a mesh axis runs over, the one named last changes fastest.
Arguments:
- tile_values: bfloat16 [2048, 128, 128], P(('row', 'col')), may hold values from -0.1875 to 0.1875
- slot_codes: int32 [2048], P(('row', 'col')), may hold values from -1 to 127, as said below
- right_start: float32 [8192, 256], P(('row', 'col')), may hold values from -6 to 6
- left_start: float32 [8192, 256], P(('row', 'col')), may hold values from -6 to 6
- node_diagonal: float32 [8192], P(('row', 'col')), may hold values from 1 to 3
- row_scale: float32 [8192], P(('row', 'col')), may hold values from 0.2 to 15
Outputs:
- right_block: float32 [8192, 256], P(('row', 'col'))
- left_block: float32 [8192, 256], P(('row', 'col'))
- projections: float32 [2, 256, 256], replicated
The draws below stay inside these ranges and needn't reach their ends.
Inputs may be any that keep to these rules, and one draw needn't show every extreme that they name: `slot_codes`: slot (s, p, c) carries a tile that device s extracted for owner p; its code is -1 (empty) or a position a 16 + b in p's block grid of 8 x 2 * 8 places. The codes of one owner's live slots over all sources are distinct, so an owner receives at most 32 live tiles, and some owner receives exactly 32. A source fills at most 2 slots for one owner, and some source fills all 2.
All inputs are finite; a program needn't handle non-finite values.
Results may differ from the reference program's by a relative error of at most 0.002.
Values may be sent and summed in bfloat16 or wider, within the bound.
No kernel may reach another device: no remote copies, remote signals or barrier semaphores. Data moves between devices by JAX's collectives and lax.ppermute only.
A program may use at most 128 MiB of HBM per device.

```python
import math
import jax
import jax.numpy as jnp
from jax import lax

TILE = 128
PORTS = 256
CAP = 2
ITERS = 2
OWNERS = 32
ORDER = 8192
N_ROW = 8
N_COL = 4


def permute_one(sub_key):
    return jax.random.permutation(sub_key, N_ROW * N_COL)


def permute_places(sub_key):
    return jax.random.permutation(sub_key, 4 * N_ROW * N_COL)


def draw_slot_codes(key, part):
    owners = N_ROW * N_COL
    key_busy = jax.random.fold_in(key, 11)
    key_forced = jax.random.fold_in(key, 12)
    key_light = jax.random.fold_in(key, 13)
    key_order = jax.random.fold_in(key, 14)
    key_place = jax.random.fold_in(key, 15)
    busy = jax.random.randint(key_busy, (owners,), 0, 8) == 0
    forced = jax.random.randint(key_forced, (), 0, owners)
    busy = jnp.logical_or(busy, jnp.arange(owners) == forced)
    light = jax.random.randint(key_light, (owners, owners), 0, 2)
    source_order = jax.vmap(permute_one)(jax.random.split(key_order, owners))
    source_rank = jnp.argsort(source_order, axis=1)
    heavy = jnp.where(source_rank < owners // 2, CAP, 0)
    counts = jnp.where(busy[:, None], heavy, light).astype(jnp.int32)
    starts = jnp.cumsum(counts, axis=1) - counts
    places = jax.vmap(permute_places)(jax.random.split(key_place, owners))
    slot_ids = jnp.arange(CAP, dtype=jnp.int32)
    index = starts[:, :, None] + slot_ids[None, None, :]
    live = slot_ids[None, None, :] < counts[:, :, None]
    safe_index = jnp.where(live, index, 0)
    picked = jnp.take_along_axis(places, safe_index.reshape(owners, owners * CAP), axis=1)
    codes = jnp.where(live, picked.reshape(owners, owners, CAP), -1)
    return jnp.transpose(codes, (1, 0, 2)).reshape(owners * owners * CAP).astype(jnp.int32)


def draw_row_scale(key, part):
    position = jnp.arange(ORDER).astype(jnp.float32)
    trend = jnp.exp(math.log(3.0) * position / ORDER)
    lower, upper = (math.log(0.3), math.log(3.0))
    spread = jax.random.uniform(key, (ORDER,), jnp.float32, lower, upper)
    return (jnp.exp(spread) * trend).astype(jnp.float32)


def block_levels(stream_key, shape, shards, low, largest):
    def one(dim, parts):
        steps = jax.random.uniform(jax.random.fold_in(jax.random.fold_in(stream_key, 6), dim), (parts,), jnp.float32, low / len(shards), largest / len(shards))
        return jnp.repeat(jnp.exp(steps), shape[dim] // parts).reshape((-1,) + (1,) * (len(shape) - dim - 1))

    factor_of = one(*shards[0])
    for cut in shards[1:]:
        factor_of = factor_of * one(*cut)
    return factor_of


def bell_draw(key, extent, width, bound, cuts=(), kind=jnp.bfloat16):
    gain = block_levels(key, extent, cuts, -0.22, 0.18) if cuts else 1.0
    array = jax.random.normal(key, extent, jnp.float32) * width * gain
    return jnp.minimum(jnp.maximum(array, -bound), bound).astype(kind)


def setup_inputs(seed: int = 0) -> dict:
    streams_of = jax.random.split(jax.random.key(seed), 7)
    return {
        "tile_values": bell_draw(streams_of[0], (OWNERS * OWNERS * CAP, TILE, TILE), (TILE * OWNERS // 4) ** -0.5, 0.1875, ((0, 32),)),
        "slot_codes": draw_slot_codes(jax.random.fold_in(streams_of[6], 71), 0),
        "right_start": bell_draw(streams_of[2], (ORDER, PORTS), 1.0, 6.0, ((0, 32),), jnp.float32),
        "left_start": bell_draw(streams_of[3], (ORDER, PORTS), 0.7, 6.0, ((0, 32),), jnp.float32),
        "node_diagonal": jnp.clip(1.0 + 2.0 * jax.random.uniform(streams_of[4], (ORDER,), jnp.float32) ** block_levels(streams_of[4], (ORDER,), ((0, 32),), -0.2, 0.2), 1.0, 3.0),
        "row_scale": draw_row_scale(jax.random.fold_in(streams_of[6], 71), 0),
    }


epsilon = 1e-06

def region_matrix(stacked_tiles, stacked_codes, owner_id, owners):
    places = 4 * owners
    slot_tiles = stacked_tiles[:, owner_id].reshape(owners * CAP, TILE, TILE)
    slot_keys = stacked_codes[:, owner_id].reshape(owners * CAP)
    safe_keys = jnp.where(slot_keys >= 0, slot_keys, places).astype(jnp.int32)
    region = jnp.zeros((places, TILE, TILE), jnp.float32)
    region = region.at[safe_keys].set(slot_tiles.astype(jnp.float32), mode='drop')
    region = region.reshape(2 * N_COL, 2 * N_ROW, TILE, TILE).transpose(0, 2, 1, 3)
    return region.reshape(2 * N_COL * TILE, 2 * N_ROW * TILE)

def apply_tiles(stacked_tiles, stacked_codes, right_bf, left_bf):
    owners = N_ROW * N_COL
    right_four = right_bf.reshape(N_ROW, N_COL, 2 * TILE, PORTS)
    left_four = left_bf.reshape(N_ROW, N_COL, 2 * TILE, PORTS)

    def accumulate(carry, owner_id):
        right_full, left_full = carry
        row_index = owner_id // N_COL
        col_index = owner_id % N_COL
        matrix = region_matrix(stacked_tiles, stacked_codes, owner_id, owners)
        right_cols = right_four[:, col_index].reshape(2 * N_ROW * TILE, PORTS).astype(jnp.float32)
        right_part = jnp.dot(matrix, right_cols, precision=lax.Precision.HIGHEST)
        right_full = right_full.at[row_index].add(right_part.reshape(N_COL, 2 * TILE, PORTS))
        left_rows = left_four[row_index].reshape(2 * N_COL * TILE, PORTS).astype(jnp.float32)
        left_part = jnp.dot(matrix.T, left_rows, precision=lax.Precision.HIGHEST)
        left_full = left_full.at[:, col_index].add(left_part.reshape(N_ROW, 2 * TILE, PORTS))
        return ((right_full, left_full), None)
    start = jnp.zeros((N_ROW, N_COL, 2 * TILE, PORTS), jnp.float32)
    (right_full, left_full), _ = lax.scan(accumulate, (start, start), jnp.arange(owners, dtype=jnp.int32))
    return (right_full.reshape(ORDER, PORTS), left_full.reshape(ORDER, PORTS))

def reference(tile_values, slot_codes, right_start, left_start, node_diagonal, row_scale):
    owners = N_ROW * N_COL
    stacked_tiles = tile_values.reshape(owners, owners, CAP, TILE, TILE)
    stacked_codes = slot_codes.reshape(owners, owners, CAP)
    scale_col = row_scale[:, None]
    diag_col = node_diagonal[:, None]
    right_vec = right_start
    left_vec = right_start + left_start
    stored = []
    for turn in range(ITERS):
        right_bf = right_vec.astype(jnp.bfloat16)
        scaled_left = scale_col * left_vec
        left_bf = scaled_left.astype(jnp.bfloat16)
        right_prod, left_prod = apply_tiles(stacked_tiles, stacked_codes, right_bf, left_bf)
        right_new = scale_col * (right_prod + diag_col * right_vec)
        left_new = left_prod + diag_col * scaled_left
        project = jnp.dot(left_vec.T, right_new, precision=lax.Precision.HIGHEST) / ORDER
        right_rest = right_new - jnp.dot(right_vec, project, precision=lax.Precision.HIGHEST)
        left_rest = left_new - jnp.dot(left_vec, project.T, precision=lax.Precision.HIGHEST)
        right_norm = jnp.sqrt(lax.optimization_barrier(jnp.sum(right_rest * right_rest, axis=0)) / ORDER + epsilon)
        left_norm = jnp.sqrt(lax.optimization_barrier(jnp.sum(left_rest * left_rest, axis=0)) / ORDER + epsilon)
        right_vec = right_rest / right_norm[None, :]
        left_vec = left_rest / left_norm[None, :]
        stored.append(project)
    return (right_vec, left_vec, jnp.stack(stored))
```

```python
import jax
import jax.numpy as jnp
from jax import lax
from jax.sharding import PartitionSpec as P

ITERS = 2


epsilon = 1e-06


AXES = ("row", "col")


def copies_of_all(piece):
    owners = lax.axis_size("row") * lax.axis_size("col")
    copies = jnp.broadcast_to(piece[None], (owners,) + piece.shape)
    return lax.all_to_all(copies, AXES, split_axis=0, concat_axis=0, tiled=True)


def sum_over_all(whole):
    owners = lax.axis_size("row") * lax.axis_size("col")
    pieces = whole.reshape(owners, whole.shape[0] // owners, whole.shape[1])
    piece = jnp.sum(lax.all_to_all(pieces, AXES, split_axis=0, concat_axis=0, tiled=True), axis=0)
    return copies_of_all(piece).reshape(whole.shape)


def local(tile_values, slot_codes, right_start, left_start, node_diagonal, row_scale):
    row_size = lax.axis_size("row")
    col_size = lax.axis_size("col")
    owners = row_size * col_size
    tile_rows = tile_values.shape[1]
    order_rows = right_start.shape[0] * owners
    grid_rows = 2 * col_size
    grid_cols = 2 * row_size
    got_tiles, got_codes = (
        lax.all_to_all(tile_values, ("row", "col"), split_axis=0, concat_axis=0, tiled=True),
        lax.all_to_all(slot_codes, ("row", "col"), split_axis=0, concat_axis=0, tiled=True),
    )
    live = got_codes >= 0
    places = grid_rows * grid_cols
    safe_keys = jnp.where(live, got_codes, places)
    region = jnp.zeros((places, tile_rows, tile_rows), jnp.bfloat16)
    region = region.at[safe_keys].set(got_tiles, mode="drop")
    region = region.reshape(grid_rows, grid_cols, tile_rows, tile_rows).transpose(0, 2, 1, 3)
    matrix = region.reshape(grid_rows * tile_rows, grid_cols * tile_rows)
    scale_col = row_scale[:, None]
    diag_col = node_diagonal[:, None]
    right_vec = right_start
    left_vec = right_start + left_start
    stored = []
    for turn in range(ITERS):
        right_bf = right_vec.astype(jnp.bfloat16)
        scaled_left = scale_col * left_vec
        left_bf = scaled_left.astype(jnp.bfloat16)
        right_cols = lax.all_gather(right_bf, "row", axis=0, tiled=True)
        left_rows = lax.all_gather(left_bf, "col", axis=0, tiled=True)
        right_part = jnp.dot(matrix, right_cols, preferred_element_type=jnp.float32)
        left_part = lax.dot_general(
            matrix, left_rows, (((0,), (0,)), ((), ())), preferred_element_type=jnp.float32
        )
        right_prod = lax.psum_scatter(right_part, "col", scatter_dimension=0, tiled=True)
        left_prod = lax.psum_scatter(left_part, "row", scatter_dimension=0, tiled=True)
        right_new = scale_col * (right_prod + diag_col * right_vec)
        left_new = left_prod + diag_col * scaled_left
        local_proj = jnp.dot(left_vec.T, right_new, precision=lax.Precision.HIGHEST)
        project = sum_over_all(local_proj) / order_rows
        right_rest = right_new - jnp.dot(right_vec, project, precision=lax.Precision.HIGHEST)
        left_rest = left_new - jnp.dot(left_vec, project.T, precision=lax.Precision.HIGHEST)
        squares = jnp.stack([jnp.sum(right_rest * right_rest, axis=0), jnp.sum(left_rest * left_rest, axis=0)])
        right_sq, left_sq = jnp.sum(copies_of_all(squares), axis=0)
        right_vec = right_rest / jnp.sqrt(right_sq / order_rows + epsilon)[None, :]
        left_vec = left_rest / jnp.sqrt(left_sq / order_rows + epsilon)[None, :]
        stored.append(project)
    return (right_vec, left_vec, jnp.stack(stored))


def solution(mesh):
    return jax.shard_map(
        local,
        mesh=mesh,
        in_specs=(
            P(("row", "col"), None, None),
            P(("row", "col")),
            P(("row", "col"), None),
            P(("row", "col"), None),
            P(("row", "col")),
            P(("row", "col")),
        ),
        out_specs=(P(("row", "col"), None), P(("row", "col"), None), P()),
        check_vma=False,
    )
```

```python
import jax
import jax.numpy as jnp
from jax import lax
from jax.experimental import pallas as pl
from jax.experimental.pallas import tpu as pltpu
from jax.sharding import PartitionSpec as P


ITERS = 2
AXES = ("row", "col")

epsilon = 1e-06
bf16 = jnp.bfloat16
f32 = jnp.float32
FIRST = (((0,), (0,)), ((), ()))


def partner(value, axis, offset):
    size = lax.axis_size(axis)
    return lax.ppermute(value, axis, [(index, index ^ offset) for index in range(size)])


def copies_of_all(piece):
    owners = lax.axis_size("row") * lax.axis_size("col")
    copies = jnp.broadcast_to(piece[None], (owners,) + piece.shape)
    return lax.all_to_all(copies, AXES, split_axis=0, concat_axis=0, tiled=True)


def sum_over_all(whole):
    owners = lax.axis_size("row") * lax.axis_size("col")
    pieces = whole.reshape(owners, whole.shape[0] // owners, whole.shape[1])
    slices = lax.all_to_all(pieces, AXES, split_axis=0, concat_axis=0, tiled=True)
    piece = jnp.sum(slices, axis=0)
    return copies_of_all(piece).reshape(whole.shape)


def assemble(tiles, codes, place, levels, col_size):
    slots, tile, _ = tiles.shape
    grid_cols = 4 * levels
    cap = slots // (2 * levels * col_size)
    shape = jax.ShapeDtypeStruct((2 * col_size * tile, 2 * levels * tile), tiles.dtype)

    def kernel(code_ref, place_ref, tile_ref, own_ref, sib_ref):
        level, core, col = place_ref[0], place_ref[1], place_ref[2]
        me = (level * 2 + core) * col_size + col
        own_ref[...] = jnp.zeros_like(own_ref)
        sib_ref[...] = jnp.zeros_like(sib_ref)

        def put(slot, carry):
            source = slot // cap
            source_row = source // col_size
            near = ((source_row // 2) ^ level) * 2 + ((source_row % 2) ^ core)
            near = near * col_size + ((source % col_size) ^ col)
            code = code_ref[near * slots + me * cap + slot % cap]

            @pl.when(code >= 0)
            def _():
                block_row = code // grid_cols
                block_col = code % grid_cols
                owner_row = block_col // 2
                down = ((block_row // 2) ^ col) * 2 + block_row % 2
                across = ((owner_row // 2) ^ level) * 2 + block_col % 2
                rows = pl.ds(pl.multiple_of(down * tile, tile), tile)
                cols = pl.ds(pl.multiple_of(across * tile, tile), tile)

                @pl.when(owner_row % 2 == core)
                def _():
                    own_ref[rows, cols] = tile_ref[slot]

                @pl.when(owner_row % 2 != core)
                def _():
                    sib_ref[rows, cols] = tile_ref[slot]

            return carry

        lax.fori_loop(0, slots, put, 0)

    return pl.pallas_call(
        kernel,
        out_shape=(shape, shape),
        in_specs=[
            pl.BlockSpec(memory_space=pltpu.SMEM),
            pl.BlockSpec(memory_space=pltpu.SMEM),
            pl.BlockSpec(memory_space=pltpu.VMEM),
        ],
        name="assemble",
    )(codes, place, tiles)


def project_part(left, right, extra):
    rows, ports = left[0].shape

    def kernel(*refs):
        lefts, rights, extra_ref, out_ref = refs[:2], refs[2:4], refs[4], refs[5]
        total = extra_ref[...]
        for left_ref, right_ref in zip(lefts, rights):
            for start in range(0, rows, ports):
                part = right_ref[start : start + ports]
                high = part.astype(bf16)
                low = (part - high.astype(f32)).astype(bf16)
                weight = left_ref[start : start + ports]
                total += lax.dot_general(weight, high, FIRST, preferred_element_type=f32)
                total += lax.dot_general(weight, low, FIRST, preferred_element_type=f32)
        out_ref[...] = total

    return pl.pallas_call(
        kernel, out_shape=jax.ShapeDtypeStruct((ports, ports), f32), name="project_part"
    )(*left, *right, extra)


def local(tile_values, slot_codes, right_start, left_start, node_diagonal, row_scale):
    row_size = lax.axis_size("row")
    col_size = lax.axis_size("col")
    levels = row_size // 2
    rows = right_start.shape[0]
    order_rows = rows * row_size * col_size
    row_index = lax.axis_index("row")
    place = jnp.stack([row_index // 2, row_index % 2, lax.axis_index("col")]).astype(jnp.int32)

    def gather(right, left):
        right_all = jnp.concatenate(
            [right] + [partner(right, "row", 2 * k) for k in range(1, levels)], axis=0
        )
        left_own = jnp.concatenate([left] + [partner(left, "col", k) for k in range(1, col_size)], axis=0)
        return right_all, left_own, partner(left_own, "row", 1)

    scale_col = row_scale[:, None]
    diag_col = node_diagonal[:, None]
    right_vec = right_start
    left_vec = right_start + left_start
    stored = []
    for turn in range(ITERS):
        right_bf = right_vec.astype(bf16)
        scaled_left = scale_col * left_vec
        left_bf = scaled_left.astype(bf16)
        diag_right = diag_col * right_vec
        local_proj = lax.dot_general(scaled_left, diag_right, FIRST, precision=lax.Precision.HIGHEST)
        right_all, left_own, left_sib = gather(right_bf, left_bf)
        if turn == 0:
            got_tiles = lax.all_to_all(tile_values, AXES, split_axis=0, concat_axis=0, tiled=True)
            codes = slot_codes
            for axis, offsets in (
                ("col", range(1, col_size)),
                ("row", (1,)),
                ("row", range(2, row_size, 2)),
            ):
                codes = jnp.concatenate([codes] + [partner(codes, axis, k) for k in offsets])
            got_tiles, codes, right_all, left_own, left_sib = lax.optimization_barrier(
                (got_tiles, codes, right_all, left_own, left_sib)
            )
            own_half, sib_half = assemble(got_tiles, codes, place, levels, col_size)
            other_half = partner(sib_half, "row", 1)
        left_part = lax.dot_general(own_half, left_own, FIRST, preferred_element_type=f32) + lax.dot_general(
            other_half, left_sib, FIRST, preferred_element_type=f32
        )
        left_part, right_all = lax.optimization_barrier((left_part, right_all))
        right_own = jnp.dot(own_half, right_all, preferred_element_type=f32)
        right_sib = jnp.dot(other_half, right_all, preferred_element_type=f32)
        left_prod = left_part[:rows]
        for k in range(1, levels):
            left_prod += partner(left_part[k * rows : (k + 1) * rows], "row", 2 * k)
        project = project_part((left_own, left_sib), (right_own, right_sib), local_proj)
        project = sum_over_all(project) / order_rows
        right_got = partner(right_sib, "row", 1)
        right_pair = right_own + right_got
        right_prod = right_pair[:rows]
        for k in range(1, col_size):
            right_prod += partner(right_pair[k * rows : (k + 1) * rows], "col", k)
        right_new = scale_col * (right_prod + diag_right)
        left_new = left_prod + diag_col * scaled_left
        right_rest = right_new - jnp.dot(right_vec, project, precision=lax.Precision.HIGHEST)
        left_rest = left_new - jnp.dot(left_vec, project.T, precision=lax.Precision.HIGHEST)
        squares = jnp.stack(
            [jnp.sum(right_rest * right_rest, axis=0), jnp.sum(left_rest * left_rest, axis=0)]
        )
        right_sq, left_sq = jnp.sum(copies_of_all(squares), axis=0)
        right_vec = right_rest / jnp.sqrt(right_sq / order_rows + epsilon)[None, :]
        left_vec = left_rest / jnp.sqrt(left_sq / order_rows + epsilon)[None, :]
        stored.append(project)
    return (right_vec, left_vec, jnp.stack(stored))


def solution(mesh):
    return jax.shard_map(
        local,
        mesh=mesh,
        in_specs=(
            P(AXES, None, None),
            P(AXES),
            P(AXES, None),
            P(AXES, None),
            P(AXES),
            P(AXES),
        ),
        out_specs=(P(AXES, None), P(AXES, None), P()),
        check_vma=False,
    )
```

```python
import jax
import jax.numpy as jnp
from jax import lax
from jax.experimental import pallas as pl
from jax.experimental.pallas import tpu as pltpu
from jax.sharding import PartitionSpec as P


ITERS = 2
AXES = ("row", "col")

epsilon = 1e-06
VMEM_BYTES = 4 * 2**20
bf16 = jnp.bfloat16
f32 = jnp.float32
FIRST = (((0,), (0,)), ((), ()))


def in_vmem(*arrays):
    if sum(array.size * array.dtype.itemsize for array in arrays) > VMEM_BYTES:
        return arrays
    return tuple(pltpu.with_memory_space_constraint(array, pltpu.VMEM) for array in arrays)


def partner(value, axis, offset):
    size = lax.axis_size(axis)
    return lax.ppermute(value, axis, [(index, index ^ offset) for index in range(size)])


def copies_of_all(piece):
    owners = lax.axis_size("row") * lax.axis_size("col")
    copies = jnp.broadcast_to(piece[None], (owners,) + piece.shape)
    return lax.all_to_all(copies, AXES, split_axis=0, concat_axis=0, tiled=True)


def sum_over_all(whole):
    owners = lax.axis_size("row") * lax.axis_size("col")
    pieces = whole.reshape(owners, whole.shape[0] // owners, whole.shape[1])
    slices = lax.all_to_all(pieces, AXES, split_axis=0, concat_axis=0, tiled=True)
    piece = jnp.sum(slices, axis=0)
    return copies_of_all(piece).reshape(whole.shape)


def bits_of(size):
    return size.bit_length() - 1


def reverse_bits(value, count):
    return sum(((value >> bit) & 1) << (count - 1 - bit) for bit in range(count))


def assemble(tiles, codes, place, levels, col_size):
    slots, tile, _ = tiles.shape
    cap = slots // (2 * levels * col_size)
    grid_bits = bits_of(4 * levels)
    shape = jax.ShapeDtypeStruct((2 * col_size * tile, 2 * levels * tile), tiles.dtype)

    def kernel(code_ref, place_ref, tile_ref, own_ref, sib_ref):
        level, core, col = place_ref[0], place_ref[1], place_ref[2]
        mine = ((level * 2 + core) * col_size + col) * cap
        own_ref[...] = jnp.zeros_like(own_ref)
        sib_ref[...] = jnp.zeros_like(sib_ref)

        def put(slot, carry):
            source = slot >> bits_of(cap)
            source_row = source >> bits_of(col_size)
            near = ((source_row >> 1) ^ level) * 2 + ((source_row & 1) ^ core)
            near = near * col_size + ((source & (col_size - 1)) ^ col)
            code = code_ref[near * slots + mine + (slot & (cap - 1))]

            @pl.when(code >= 0)
            def _():
                block_row = code >> grid_bits
                block_col = code & ((1 << grid_bits) - 1)
                owner_row = block_col >> 1
                down = ((block_row >> 1) ^ col) * 2 + (block_row & 1)
                across = reverse_bits((owner_row >> 1) ^ level, bits_of(levels)) * 2 + (block_col & 1)
                rows = pl.ds(pl.multiple_of(down * tile, tile), tile)
                cols = pl.ds(pl.multiple_of(across * tile, tile), tile)

                @pl.when((owner_row & 1) == core)
                def _():
                    own_ref[rows, cols] = tile_ref[slot]

                @pl.when((owner_row & 1) != core)
                def _():
                    sib_ref[rows, cols] = tile_ref[slot]

            return carry

        lax.fori_loop(0, slots, put, 0, unroll=4)

    return pl.pallas_call(
        kernel,
        out_shape=(shape, shape),
        in_specs=[
            pl.BlockSpec(memory_space=pltpu.SMEM),
            pl.BlockSpec(memory_space=pltpu.SMEM),
            pl.BlockSpec(memory_space=pltpu.VMEM),
        ],
        name="assemble",
    )(codes, place, tiles)


def project_part(left_own, left_sib, right_own, right_sib, extra):
    rows, ports = left_own.shape

    def kernel(*refs):
        lefts, rights, extra_ref, out_ref = refs[:2], refs[2:4], refs[4], refs[5]
        total = extra_ref[...]
        for left_ref, right_ref in zip(lefts, rights):
            for start in range(0, rows, ports):
                part = right_ref[start : start + ports]
                high = part.astype(bf16)
                low = (part - high.astype(f32)).astype(bf16)
                weight = left_ref[start : start + ports]
                total += lax.dot_general(weight, high, FIRST, preferred_element_type=f32)
                total += lax.dot_general(weight, low, FIRST, preferred_element_type=f32)
        out_ref[...] = total

    return pl.pallas_call(
        kernel, out_shape=jax.ShapeDtypeStruct((ports, ports), f32), name="project_part"
    )(left_own, left_sib, right_own, right_sib, extra)


def local(tile_values, slot_codes, right_start, left_start, node_diagonal, row_scale):
    row_size = lax.axis_size("row")
    col_size = lax.axis_size("col")
    levels = row_size // 2
    rows = right_start.shape[0]
    order_rows = rows * row_size * col_size
    row_index = lax.axis_index("row")
    place = jnp.stack([row_index // 2, row_index % 2, lax.axis_index("col")]).astype(jnp.int32)

    def gather(right, left):
        order = [reverse_bits(k, bits_of(levels)) for k in range(levels)]
        right_all = [right] + [partner(right, "row", 2 * k) for k in order[1:]]
        left_own = jnp.concatenate([left] + [partner(left, "col", k) for k in range(1, col_size)], axis=0)
        return right_all, left_own, partner(left_own, "row", 1)

    scale_col = row_scale[:, None]
    diag_col = node_diagonal[:, None]
    right_vec = right_start
    left_vec = right_start + left_start
    stored = []
    for turn in range(ITERS):
        right_bf = right_vec.astype(bf16)
        scaled_left = scale_col * left_vec
        left_bf = scaled_left.astype(bf16)
        diag_right = diag_col * right_vec
        right_all, left_own, left_sib = gather(right_bf, left_bf)
        local_proj = lax.dot_general(scaled_left, diag_right, FIRST, precision=lax.Precision.HIGHEST)
        if turn == 0:
            got_tiles = lax.all_to_all(tile_values, AXES, split_axis=0, concat_axis=0, tiled=True)
            codes = slot_codes
            for axis, offsets in (("col", range(1, col_size)), ("row", (1,)), ("row", range(2, row_size, 2))):
                codes = jnp.concatenate([codes] + [partner(codes, axis, k) for k in offsets])
            got_tiles, codes, left_own, left_sib, local_proj = lax.optimization_barrier(
                (got_tiles, codes, left_own, left_sib, local_proj)
            )
            (got_tiles,) = in_vmem(got_tiles)
            own_half, sib_half = assemble(got_tiles, codes, place, levels, col_size)
            other_half = partner(sib_half, "row", 1)
        else:
            right_all, left_own, left_sib, local_proj = lax.optimization_barrier(
                (right_all, left_own, left_sib, local_proj)
            )
        right_all = jnp.concatenate(right_all, axis=0)
        half = levels * rows // 2

        def left_dots(cols):
            return lax.dot_general(
                own_half[:, cols], left_own, FIRST, preferred_element_type=f32
            ) + lax.dot_general(other_half[:, cols], left_sib, FIRST, preferred_element_type=f32)

        left_send = left_dots(slice(half, None))
        left_keep = left_dots(slice(0, half))
        if turn == 0:
            left_send, right_last = lax.optimization_barrier((left_send, right_all))
        else:
            left_send, right_all = lax.optimization_barrier((left_send, right_all))
            right_last = right_all
        right_own = jnp.dot(own_half, right_all, preferred_element_type=f32)
        right_sib = jnp.dot(other_half, right_last, preferred_element_type=f32)
        for bit in range(bits_of(levels)):
            left_got = partner(left_send, "row", 2 << bit)
            kept = left_keep.shape[0] // 2
            if kept >= rows:
                left_send = left_keep[kept:] + left_got[kept:]
                left_keep = left_keep[:kept] + left_got[:kept]
            else:
                left_prod = left_keep + left_got
        project = project_part(*in_vmem(left_own, left_sib, right_own, right_sib, local_proj))
        project = sum_over_all(project) / order_rows
        right_got = partner(right_sib, "row", 1)
        right_pair = right_own + right_got
        right_prod = right_pair[:rows]
        for k in range(1, col_size):
            right_prod += partner(right_pair[k * rows : (k + 1) * rows], "col", k)
        right_new = scale_col * (right_prod + diag_right)
        left_new = left_prod + diag_col * scaled_left
        right_rest = right_new - jnp.dot(right_vec, project, precision=lax.Precision.HIGHEST)
        left_rest = left_new - jnp.dot(left_vec, project.T, precision=lax.Precision.HIGHEST)
        squares = jnp.stack(
            [jnp.sum(right_rest * right_rest, axis=0), jnp.sum(left_rest * left_rest, axis=0)]
        )
        right_sq, left_sq = jnp.sum(copies_of_all(squares), axis=0)
        right_vec = right_rest / jnp.sqrt(right_sq / order_rows + epsilon)[None, :]
        left_vec = left_rest / jnp.sqrt(left_sq / order_rows + epsilon)[None, :]
        stored.append(project)
    return (right_vec, left_vec, jnp.stack(stored))


def solution(mesh):
    return jax.shard_map(
        local,
        mesh=mesh,
        in_specs=(
            P(AXES, None, None),
            P(AXES),
            P(AXES, None),
            P(AXES, None),
            P(AXES),
            P(AXES),
        ),
        out_specs=(P(AXES, None), P(AXES, None), P()),
        check_vma=False,
    )
```

```python
import jax
import jax.numpy as jnp
from jax import lax
from jax.experimental import pallas as pl
from jax.experimental.pallas import tpu as pltpu
from jax.sharding import PartitionSpec as P


ITERS = 2
AXES = ("row", "col")

epsilon = 1e-06
VMEM_BYTES = 4 * 2**20
bf16 = jnp.bfloat16
f32 = jnp.float32
FIRST = (((0,), (0,)), ((), ()))


def in_vmem(*arrays):
    if sum(array.size * array.dtype.itemsize for array in arrays) > VMEM_BYTES:
        return arrays
    return tuple(pltpu.with_memory_space_constraint(array, pltpu.VMEM) for array in arrays)


def partner(value, axis, offset):
    size = lax.axis_size(axis)
    return lax.ppermute(value, axis, [(index, index ^ offset) for index in range(size)])


def copies_of_all(piece):
    owners = lax.axis_size("row") * lax.axis_size("col")
    copies = jnp.broadcast_to(piece[None], (owners,) + piece.shape)
    return lax.all_to_all(copies, AXES, split_axis=0, concat_axis=0, tiled=True)


def sum_over_all(whole):
    owners = lax.axis_size("row") * lax.axis_size("col")
    pieces = whole.reshape(owners, whole.shape[0] // owners, whole.shape[1])
    slices = lax.all_to_all(pieces, AXES, split_axis=0, concat_axis=0, tiled=True)
    piece = jnp.sum(slices, axis=0)
    return copies_of_all(piece).reshape(whole.shape)


def bits_of(size):
    return size.bit_length() - 1


def reverse_bits(value, count):
    return sum(((value >> bit) & 1) << (count - 1 - bit) for bit in range(count))


def assemble(tiles, codes, place, levels, col_size):
    slots, tile, _ = tiles.shape
    cap = slots // (2 * levels * col_size)
    grid_bits = bits_of(4 * levels)
    shape = jax.ShapeDtypeStruct((2 * col_size * tile, 2 * levels * tile), tiles.dtype)

    def kernel(code_ref, place_ref, tile_ref, own_ref, sib_ref):
        level, core, col = place_ref[0], place_ref[1], place_ref[2]
        mine = ((level * 2 + core) * col_size + col) * cap
        own_ref[...] = jnp.zeros_like(own_ref)
        sib_ref[...] = jnp.zeros_like(sib_ref)

        def put(slot, carry):
            source = slot >> bits_of(cap)
            source_row = source >> bits_of(col_size)
            near = ((source_row >> 1) ^ level) * 2 + ((source_row & 1) ^ core)
            near = near * col_size + ((source & (col_size - 1)) ^ col)
            code = code_ref[near * slots + mine + (slot & (cap - 1))]

            @pl.when(code >= 0)
            def _():
                block_row = code >> grid_bits
                block_col = code & ((1 << grid_bits) - 1)
                owner_row = block_col >> 1
                down = ((block_row >> 1) ^ col) * 2 + (block_row & 1)
                across = reverse_bits((owner_row >> 1) ^ level, bits_of(levels)) * 2 + (block_col & 1)
                rows = pl.ds(pl.multiple_of(down * tile, tile), tile)
                cols = pl.ds(pl.multiple_of(across * tile, tile), tile)

                @pl.when((owner_row & 1) == core)
                def _():
                    own_ref[rows, cols] = tile_ref[slot]

                @pl.when((owner_row & 1) != core)
                def _():
                    sib_ref[rows, cols] = tile_ref[slot]

            return carry

        lax.fori_loop(0, slots, put, 0, unroll=4)

    return pl.pallas_call(
        kernel,
        out_shape=(shape, shape),
        in_specs=[
            pl.BlockSpec(memory_space=pltpu.SMEM),
            pl.BlockSpec(memory_space=pltpu.SMEM),
            pl.BlockSpec(memory_space=pltpu.VMEM),
        ],
        name="assemble",
    )(codes, place, tiles)


def project_part(left_own, left_sib, right_own, right_sib, extra):
    rows, ports = left_own.shape

    def kernel(*refs):
        lefts, rights, extra_ref, out_ref = refs[:2], refs[2:4], refs[4], refs[5]
        total = extra_ref[...]
        for left_ref, right_ref in zip(lefts, rights):
            for start in range(0, rows, ports):
                part = right_ref[start : start + ports]
                high = part.astype(bf16)
                low = (part - high.astype(f32)).astype(bf16)
                weight = left_ref[start : start + ports]
                total += lax.dot_general(weight, high, FIRST, preferred_element_type=f32)
                total += lax.dot_general(weight, low, FIRST, preferred_element_type=f32)
        out_ref[...] = total

    return pl.pallas_call(
        kernel, out_shape=jax.ShapeDtypeStruct((ports, ports), f32), name="project_part"
    )(left_own, left_sib, right_own, right_sib, extra)


def local(tile_values, slot_codes, right_start, left_start, node_diagonal, row_scale):
    row_size = lax.axis_size("row")
    col_size = lax.axis_size("col")
    levels = row_size // 2
    rows = right_start.shape[0]
    order_rows = rows * row_size * col_size
    row_index = lax.axis_index("row")
    place = jnp.stack([row_index // 2, row_index % 2, lax.axis_index("col")]).astype(jnp.int32)

    def gather(right, left):
        order = [reverse_bits(k, bits_of(levels)) for k in range(levels)]
        right_all = [right] + [partner(right, "row", 2 * k) for k in order[1:]]
        left_own = jnp.concatenate([left] + [partner(left, "col", k) for k in range(1, col_size)], axis=0)
        return right_all, left_own, partner(left_own, "row", 1)

    scale_col = row_scale[:, None]
    diag_col = node_diagonal[:, None]
    right_vec = right_start
    left_vec = right_start + left_start
    stored = []
    for turn in range(ITERS):
        right_bf = right_vec.astype(bf16)
        scaled_left = scale_col * left_vec
        left_bf = scaled_left.astype(bf16)
        diag_right = diag_col * right_vec
        right_all, left_own, left_sib = gather(right_bf, left_bf)
        local_proj = lax.dot_general(scaled_left, diag_right, FIRST, precision=lax.Precision.HIGH)
        if turn == 0:
            got_tiles = lax.all_to_all(tile_values, AXES, split_axis=0, concat_axis=0, tiled=True)
            codes = slot_codes
            for axis, offsets in (("col", range(1, col_size)), ("row", (1,)), ("row", range(2, row_size, 2))):
                codes = jnp.concatenate([codes] + [partner(codes, axis, k) for k in offsets])
            got_tiles, codes, left_own, left_sib, local_proj = lax.optimization_barrier(
                (got_tiles, codes, left_own, left_sib, local_proj)
            )
            (got_tiles,) = in_vmem(got_tiles)
            own_half, sib_half = assemble(got_tiles, codes, place, levels, col_size)
            other_half = partner(sib_half, "row", 1)
        right_all = jnp.concatenate(right_all, axis=0)
        half = levels * rows // 2

        def left_dots(cols):
            return lax.dot_general(
                own_half[:, cols], left_own, FIRST, preferred_element_type=f32
            ) + lax.dot_general(other_half[:, cols], left_sib, FIRST, preferred_element_type=f32)

        left_send = left_dots(slice(half, None))
        left_keep = left_dots(slice(0, half))
        if turn == 0:
            left_send, right_last = lax.optimization_barrier((left_send, right_all))
        else:
            left_send, right_all = lax.optimization_barrier((left_send, right_all))
            right_last = right_all
        right_own = jnp.dot(own_half, right_all, preferred_element_type=f32)
        right_sib = jnp.dot(other_half, right_last, preferred_element_type=f32)
        for bit in range(bits_of(levels)):
            left_got = partner(left_send, "row", 2 << bit)
            kept = left_keep.shape[0] // 2
            if kept >= rows:
                left_send = left_keep[kept:] + left_got[kept:]
                left_keep = left_keep[:kept] + left_got[:kept]
            else:
                left_prod = left_keep + left_got
        project = project_part(*in_vmem(left_own, left_sib, right_own, right_sib, local_proj))
        project = sum_over_all(project) / order_rows
        right_got = partner(right_sib, "row", 1)
        right_pair = right_own + right_got
        right_prod = right_pair[:rows]
        for k in range(1, col_size):
            right_prod += partner(right_pair[k * rows : (k + 1) * rows], "col", k)
        right_new = scale_col * (right_prod + diag_right)
        left_new = left_prod + diag_col * scaled_left
        right_rest = right_new - jnp.dot(right_vec, project, precision=lax.Precision.HIGH)
        left_rest = left_new - jnp.dot(left_vec, project.T, precision=lax.Precision.HIGH)
        squares = jnp.stack(
            [jnp.sum(right_rest * right_rest, axis=0), jnp.sum(left_rest * left_rest, axis=0)]
        )
        right_sq, left_sq = jnp.sum(copies_of_all(squares), axis=0)
        right_vec = right_rest / jnp.sqrt(right_sq / order_rows + epsilon)[None, :]
        left_vec = left_rest / jnp.sqrt(left_sq / order_rows + epsilon)[None, :]
        stored.append(project)
    return (right_vec, left_vec, jnp.stack(stored))


def solution(mesh):
    return jax.shard_map(
        local,
        mesh=mesh,
        in_specs=(
            P(AXES, None, None),
            P(AXES),
            P(AXES, None),
            P(AXES, None),
            P(AXES),
            P(AXES),
        ),
        out_specs=(P(AXES, None), P(AXES, None), P()),
        check_vma=False,
    )
```
